32 devices in a mesh: lat: 8 (over z, y), rad: 4 (over x, core).
Axes of the slice: x: 2, y: 2, z: 4, core: 2. Of those that a mesh axis runs over, the one named last changes fastest.
Arguments:
- source: float32 [128, 32768], P('rad', 'lat'), may hold values from -6 to 6
- to_modes: float32 [128, 128], replicated, may hold values from -0.5 to 0.5
- from_modes: float32 [128, 128], replicated, may hold values from -0.5 to 0.5
- eigenvalue: float32 [128], replicated, may hold values from 0.1 to 20
- shifts: float32 [32768], P('lat'), may hold values from 0.5 to 2
- weights: float32 [31, 32768], P(None, 'lat'), may hold values from 0.02 to 0.12
- neighbors: int32 [31, 256], P(None, 'lat'), may hold values from -8 to 8, as said below
Outputs:
- smoothed: float32 [128, 32768], P('rad', 'lat')
- residual_norm: float32 [128], P('rad')
The draws below stay inside these ranges and needn't reach their ends.
Inputs may be any that keep to these rules, and one draw needn't show every extreme that they name: `neighbors`: every entry is nonzero; some entry equals -8.
All inputs are finite; a program needn't handle non-finite values.
Results may differ from the reference program's by a relative error of at most 0.000073.
Values sent between devices are 32-bit elements; how exact they have to be, the bound alone decides.
A program may use at most 64 MiB of HBM per device.

```python
import math
import jax
import jax.numpy as jnp
from jax import lax

LEVELS = 128
STENCIL = 31
BLOCK = 128
HALO_BLOCKS = 8
NODES = 32768


def draw_neighbors(key, part):
    offsets = jax.random.randint(key, (STENCIL, NODES // BLOCK), -HALO_BLOCKS, HALO_BLOCKS + 1).astype(jnp.int32)
    offsets = jnp.where(offsets == 0, HALO_BLOCKS, offsets)
    offsets = offsets.at[0, 0].set(-HALO_BLOCKS)
    return offsets.astype(jnp.int32)


def shard_levels(rng, shape, split, smallest, largest):
    factor_of = 1.0
    for dim, parts in split:
        draws = jax.random.uniform(jax.random.fold_in(jax.random.fold_in(rng, 6), dim), (parts,), jnp.float32, smallest / len(split), largest / len(split))
        factor_of = factor_of * jnp.repeat(jnp.exp(draws), shape[dim] // parts).reshape((-1,) + (1,) * (len(shape) - 1 - dim))
    return factor_of


def scatter_about(stream_key, extent, width, most, split=(), held_as=jnp.bfloat16):
    values = jax.random.normal(stream_key, extent, jnp.float32) * width
    if len(split) > 0:
        values = shard_levels(stream_key, extent, split, -0.22, 0.18) * values
    return jnp.clip(values, min=-most, max=most).astype(held_as)


def setup_inputs(seed: int = 0) -> dict:
    key_list = jax.random.split(jax.random.key(seed), 8)
    return {
        "source": scatter_about(key_list[0], (LEVELS, NODES), 1.0, 6.0, ((0, 4), (1, 8)), jnp.float32),
        "to_modes": scatter_about(key_list[1], (LEVELS, LEVELS), LEVELS ** -0.5, 0.5, (), jnp.float32),
        "from_modes": scatter_about(key_list[2], (LEVELS, LEVELS), LEVELS ** -0.5, 0.5, (), jnp.float32),
        "eigenvalue": jnp.clip(jnp.exp(jax.random.uniform(key_list[3], (LEVELS,), jnp.float32, math.log(0.1), math.log(20.0))), 0.1, 20.0),
        "shifts": jnp.clip(0.5 + 1.5 * jax.random.uniform(key_list[4], (NODES,), jnp.float32) ** shard_levels(key_list[4], (NODES,), ((0, 8),), -0.2, 0.2), 0.5, 2.0),
        "weights": jnp.clip(0.02 + 0.09999999776482582 * jax.random.uniform(key_list[5], (STENCIL, NODES), jnp.float32) ** shard_levels(key_list[5], (STENCIL, NODES), ((1, 8),), -0.2, 0.2), 0.02, 0.12),
        "neighbors": draw_neighbors(jax.random.fold_in(key_list[7], 71), 0),
    }


def operate(field, eigenvalue, shifts, weights, neighbors):
    total = lax.optimization_barrier(jnp.sum(weights, axis=0))
    coeffs = (shifts + total)[None, :] + eigenvalue[:, None]
    result = coeffs * field
    node_count = field.shape[1]
    node_ids = jnp.arange(node_count, dtype=jnp.int32)
    block_ids = (node_ids // BLOCK).astype(jnp.int32)
    lane_ids = (node_ids % BLOCK).astype(jnp.int32)
    for slot_index in range(weights.shape[0]):
        block_off = jnp.take(neighbors[slot_index].astype(jnp.int32), block_ids)
        target = (((block_ids + block_off) * BLOCK + (lane_ids + slot_index) % BLOCK) % node_count).astype(jnp.int32)
        result = result - weights[slot_index][None, :] * jnp.take(field, target, axis=1)
    return result

def reference(source, to_modes, from_modes, eigenvalue, shifts, weights, neighbors):
    modal = jnp.dot(to_modes, source, precision=lax.Precision.HIGHEST, preferred_element_type=jnp.float32)
    image = operate(modal, eigenvalue, shifts, weights, neighbors)
    base = lax.optimization_barrier(jnp.sum(modal * modal, axis=1))
    power = lax.optimization_barrier(jnp.sum(image * image, axis=1))
    upper = 1.5 * jnp.sqrt(power / (base + 1e-06))
    lower = upper * 0.125
    center = ((upper + lower) * 0.5)[:, None]
    half_width = ((upper - lower) * 0.5)[:, None]
    sigma = center / half_width
    rho_zero = 1.0 / sigma
    rho_one = 1.0 / (2.0 * sigma - rho_zero)
    first = modal / center
    second_res = modal - image / center
    update = rho_one * rho_zero * first + 2.0 * rho_one / half_width * second_res
    iterate = first + update
    final_res = second_res - operate(update, eigenvalue, shifts, weights, neighbors)
    residual_norm = jnp.sqrt(lax.optimization_barrier(jnp.sum(final_res * final_res, axis=1)) / (base + 1e-06))
    smoothed = jnp.dot(from_modes, iterate, precision=lax.Precision.HIGHEST, preferred_element_type=jnp.float32)
    return (smoothed, residual_norm)
```

```python
import functools

import jax
import jax.numpy as jnp
from jax import lax
from jax.experimental import pallas as pl
from jax.experimental.pallas import tpu as pltpu
from jax.sharding import PartitionSpec as P

BLOCK = 128
HALO = 8
CHUNKS = 4
GROUP = 8
CORES = 2
HIGHEST = lax.Precision.HIGHEST
MESH = pl.DeviceIdType.MESH


def dot(a, b):
    return jnp.dot(a, b, precision=HIGHEST, preferred_element_type=jnp.float32)


def kernel(
    L, R, S,
    src, w_hbm, to_ref, from_ref, eig_ref, shift_ref, nbr_ref,
    out, res_ref,
    gathered, wv, wr, ext1, ext2, modal, image, eig_t, coef, part, rows, s1, s2, s3, s4,
    own_sem, w_sem, ag_send, ag_recv, h1_send, h1_recv, h2_send, h2_recv, im_send, im_recv,
    s1_send, s1_recv, s2_send, s2_recv, s3_send, s3_recv, s4_send, s4_recv,
    out_send, out_recv, out_sem,
):
    T = CHUNKS
    X = R // CORES
    slab, nodes = src.shape
    K = slab * CORES
    half = nodes // CORES
    NB = half // BLOCK
    CB = NB // T
    CW = CB * BLOCK
    E = NB + 2 * HALO
    A = -(-S // GROUP)
    lat = lax.axis_index("lat")
    rad = lax.axis_index("rad")
    core = lax.rem(rad, CORES)
    chip = lax.div(rad, CORES)
    partner = chip * CORES + (1 - core)
    left_lat = lax.rem(lat + (L - 1) * (1 - core), L)
    right_lat = lax.rem(lat + core, L)

    def order(t, c):
        return t * (1 - c) + (T - 1 - t) * c

    def own_copy(q):
        return pltpu.make_async_copy(
            src.at[:, pl.ds(pl.multiple_of(core * half + q * CW, BLOCK), CW)],
            gathered.at[q, pl.ds(pl.multiple_of(rad * slab, 8), slab), :],
            own_sem.at[q],
        )

    w_copy = pltpu.make_async_copy(
        w_hbm.at[:, pl.ds(pl.multiple_of(core * half, BLOCK), half)], wv, w_sem
    )
    for q in range(T):
        own_copy(q).start()
    w_copy.start()

    barrier = pltpu.get_barrier_semaphore()
    for j in range(1, R):
        pl.semaphore_signal(
            barrier, inc=1, device_id={"lat": lat, "rad": lax.rem(rad + j, R)}, device_id_type=MESH
        )
    other_lat = left_lat * (1 - core) + right_lat * core
    pl.semaphore_signal(
        barrier, inc=1, device_id={"lat": other_lat, "rad": partner}, device_id_type=MESH
    )
    for j in range(1, L):
        pl.semaphore_signal(
            barrier, inc=1, device_id={"lat": lax.rem(lat + j, L), "rad": rad}, device_id_type=MESH
        )
    pl.semaphore_wait(barrier, R - 1 + 1 + L - 1)

    pending = []

    def remote(src_ref, dst_ref, send, recv, lat_to, rad_to):
        copy = pltpu.make_async_remote_copy(
            src_ref=src_ref, dst_ref=dst_ref, send_sem=send, recv_sem=recv,
            device_id={"lat": lat_to, "rad": rad_to}, device_id_type=MESH,
        )
        copy.start()
        pending.append(copy)

    def arrived(dst_ref, send, recv):
        pltpu.make_async_remote_copy(
            src_ref=dst_ref, dst_ref=dst_ref, send_sem=send, recv_sem=recv,
            device_id={"lat": lat, "rad": partner}, device_id_type=MESH,
        ).wait_recv()

    def slot(q, r):
        return gathered.at[q, pl.ds(pl.multiple_of(r * slab, 8), slab), :]

    for t in range(T):
        for j in range(1, R):
            to = lax.rem(rad + j, R)
            to_core = lax.rem(to, CORES)
            q = order(t, to_core)
            remote(
                src.at[:, pl.ds(pl.multiple_of(to_core * half + q * CW, BLOCK), CW)],
                slot(q, rad), ag_send.at[t, j - 1], ag_recv.at[q, rad], lat, to,
            )

    w_copy.wait()
    row_id = lax.broadcasted_iota(jnp.int32, (A * GROUP, BLOCK), 0)
    shift_rows = shift_ref[pl.ds(pl.multiple_of(core * NB, 8), NB), :]
    rows[...] = shift_rows

    def prepare(b, carry):
        wr[b, pl.ds((A - 1) * GROUP, GROUP), :] = jnp.zeros((GROUP, BLOCK), jnp.float32)
        wr[b, pl.ds(0, S), :] = wv[:, pl.ds(pl.multiple_of(b * BLOCK, BLOCK), BLOCK)]
        tile = wr[b, pl.ds(0, A * GROUP), :]
        placed = tile
        for c in range(1, GROUP):
            placed = jnp.where(lax.rem(row_id, GROUP) == c, pltpu.roll(tile, c, 1), placed)
        wr[b, pl.ds(0, A * GROUP), :] = placed
        diagonal = jnp.sum(tile, axis=0, keepdims=True) + rows[pl.ds(b, 1), :]
        wr[b, pl.ds(A * GROUP, GROUP), :] = jnp.broadcast_to(diagonal, (GROUP, BLOCK))
        return carry

    lax.fori_loop(0, NB, prepare, 0)
    levels = to_ref.shape[0]
    eig_t[...] = jnp.transpose(jnp.broadcast_to(eig_ref[...], (levels, levels)))
    eig = pl.ds(pl.multiple_of(chip * K, 8), K)

    def halo_send(buf, q, send, recv):
        upper = lax.div(q * 2, T)
        to_lat = left_lat * (1 - upper) + right_lat * upper
        at = HALO + q * CB
        dst = at + NB * (1 - upper) - NB * upper
        remote(
            buf.at[pl.ds(at, CB)], buf.at[pl.ds(dst, CB)], send.at[q], recv.at[q], to_lat, partner
        )

    def halo_wait(buf, send, recv):
        for q in range(T):
            dst = HALO + q * CB + (NB if q * 2 < T else -NB)
            arrived(buf.at[pl.ds(dst, CB)], send.at[q], recv.at[q])

    def spread(buf, k, value):
        for a in range(1, A):
            buf[a * E + k] = pltpu.roll(value, BLOCK - a * GROUP, 1)

    def spread_halo(buf):
        def step(k, carry):
            spread(buf, k, buf[k])
            spread(buf, k + NB + HALO, buf[k + NB + HALO])
            return carry

        lax.fori_loop(0, HALO, step, 0)

    own_rows = to_ref[pl.ds(pl.multiple_of(chip * K, 8), K), :]
    for t in range(T):
        q = order(t, core)
        own_copy(q).wait()
        for j in range(1, R):
            r = lax.rem(rad + j, R)
            arrived(slot(q, r), ag_send.at[t, j - 1], ag_recv.at[q, r])
        product = dot(own_rows, gathered[q])
        for i in range(CB):
            value = product[:, i * BLOCK:(i + 1) * BLOCK]
            ext1[HALO + q * CB + i] = value
            modal[chip, q * CB + i] = value
        halo_send(ext1, q, h1_send, h1_recv)
        for i in range(CB):
            spread(ext1, HALO + q * CB + i, product[:, i * BLOCK:(i + 1) * BLOCK])
    halo_wait(ext1, h1_send, h1_recv)
    spread_halo(ext1)

    def operate(buf, b, field):
        total = None
        for c in range(GROUP):
            inner = None
            for a in range(A):
                s = a * GROUP + c
                if s < S:
                    n = nbr_ref[s, core * NB + b]
                    term = buf[a * E + HALO + b + n] * wr[b, pl.ds(s, 1), :]
                    inner = term if inner is None else inner + term
            if inner is not None:
                moved = inner if c == 0 else pltpu.roll(inner, BLOCK - c, 1)
                total = moved if total is None else total + moved
        return (wr[b, pl.ds(A * GROUP, 1), :] + eig_t[eig, :]) * field - total

    zero = jnp.zeros((K, BLOCK), jnp.float32)
    sums = (zero, zero)
    for t in range(T):
        q = order(t, core)

        def first_pass(i, carry):
            b = q * CB + i
            field = ext1[HALO + b]
            value = operate(ext1, b, field)
            ext2[HALO + b] = value
            image[chip, b] = value
            return (carry[0] + field * field, carry[1] + value * value)

        sums = lax.fori_loop(0, CB, first_pass, sums)
        for j in range(1, X):
            to = lax.rem(chip + j, X)
            remote(
                image.at[chip, pl.ds(q * CB, CB)], image.at[chip, pl.ds(q * CB, CB)],
                im_send.at[t, j - 1], im_recv.at[q, chip], lat, to * CORES + core,
            )
        halo_send(ext2, q, h2_send, h2_recv)

    ones = jnp.ones((8, BLOCK), jnp.float32)

    def lanes(values):
        return lax.dot_general(
            ones, values, (((1,), (1,)), ((), ())), precision=HIGHEST,
            preferred_element_type=jnp.float32,
        )

    def lat_send(buf, send, recv):
        for j in range(1, L):
            remote(
                buf.at[lat], buf.at[lat], send.at[j - 1], recv.at[lat], lax.rem(lat + j, L), rad
            )

    def lat_sum(buf, send, recv):
        for j in range(1, L):
            l = lax.rem(lat + j, L)
            arrived(buf.at[l], send.at[j - 1], recv.at[l])
        total = buf[0]
        for l in range(1, L):
            total = total + buf[l]
        return total

    def put(buf, at, value):
        width = value.shape[1]
        if width < BLOCK:
            value = jnp.concatenate(
                [value, jnp.zeros((8, BLOCK - width), jnp.float32)], axis=1
            )
        buf[at] = value

    put(s1, lat, lanes(jnp.concatenate(sums, axis=0)))
    lat_send(s1, s1_send, s1_recv)

    for j in range(1, X):
        other = lax.rem(chip + j, X)
        other_rows = to_ref[pl.ds(pl.multiple_of(other * K, 8), K), :]
        for q in range(T):
            product = dot(other_rows, gathered[q])
            for i in range(CB):
                modal[other, q * CB + i] = product[:, i * BLOCK:(i + 1) * BLOCK]

    s2[rad] = lat_sum(s1, s1_send, s1_recv)
    for j in range(1, R):
        remote(
            s2.at[rad], s2.at[rad], s2_send.at[j - 1], s2_recv.at[rad], lat, lax.rem(rad + j, R)
        )
    for j in range(1, R):
        r = lax.rem(rad + j, R)
        arrived(s2.at[r], s2_send.at[j - 1], s2_recv.at[r])
    for x in range(X):
        line = s2[CORES * x]
        for c in range(1, CORES):
            line = line + s2[CORES * x + c]
        column = jnp.transpose(jnp.broadcast_to(line[0:1, :], (BLOCK, BLOCK)))
        base, power = column[0:K], column[K:2 * K]
        upper = 1.5 * jnp.sqrt(power / (base + 1e-06))
        lower = upper * 0.125
        center = (upper + lower) * 0.5
        half_width = (upper - lower) * 0.5
        sigma = center / half_width
        rho_zero = 1.0 / sigma
        rho_one = 1.0 / (2.0 * sigma - rho_zero)
        second = 2.0 * rho_one / half_width
        coef[x, 0] = (1.0 + rho_one * rho_zero) / center + second
        coef[x, 1] = -second / center

    mine = jnp.concatenate(
        [
            from_ref[pl.ds(pl.multiple_of(rad * slab, 8), slab), :],
            from_ref[pl.ds(pl.multiple_of(partner * slab, 8), slab), :],
        ],
        axis=0,
    )

    def columns(q):
        return out.at[:, pl.ds(pl.multiple_of(core * half + q * CW, BLOCK), CW)]

    def their_columns(q):
        return out.at[:, pl.ds(pl.multiple_of((1 - core) * half + q * CW, BLOCK), CW)]

    def finish(t):
        q = order(t, core)
        for j in range(1, X):
            x = lax.rem(chip + j, X)
            arrived(image.at[x, pl.ds(q * CB, CB)], im_send.at[t, j - 1], im_recv.at[q, x])
        blocks = []
        for i in range(CB):
            b = q * CB + i
            blocks.append(
                jnp.concatenate(
                    [coef[x, 0] * modal[x, b] + coef[x, 1] * image[x, b] for x in range(X)], axis=0
                )
            )
        product = dot(mine, jnp.concatenate(blocks, axis=1))
        part[q, 0] = product[0:slab]
        part[q, 1] = product[slab:K]
        remote(part.at[q, 1], columns(q), out_send.at[q], out_recv.at[q], lat, partner)
        pltpu.make_async_copy(part.at[q, 0], columns(q), out_sem.at[q]).start()

    finish(0)

    halo_wait(ext2, h2_send, h2_recv)
    spread_halo(ext2)

    def spread_own(b, carry):
        spread(ext2, HALO + b, ext2[HALO + b])
        return carry

    lax.fori_loop(0, NB, spread_own, 0)

    def second_pass(b, carry):
        field = ext2[HALO + b]
        value = operate(ext2, b, field)
        final = modal[chip, b] - (coef[chip, 0] * field + coef[chip, 1] * value)
        return carry + final * final

    squares = lax.fori_loop(0, NB, second_pass, zero)
    put(s3, lat, lanes(squares))
    lat_send(s3, s3_send, s3_recv)

    for t in range(1, T):
        finish(t)

    s4[core] = lat_sum(s3, s3_send, s3_recv)
    remote(s4.at[core], s4.at[core], s4_send, s4_recv, lat, partner)
    arrived(s4.at[1 - core], s4_send, s4_recv)
    base_line = s2[CORES * chip] + s2[CORES * chip + 1]
    norm = jnp.sqrt((s4[0] + s4[1]) / (base_line + 1e-06))
    res_ref[...] = jnp.where(core == 0, norm[0:1, 0:slab], norm[0:1, slab:2 * slab])

    for q in range(T):
        pltpu.make_async_copy(part.at[q, 0], columns(q), out_sem.at[q]).wait()
        arrived(their_columns(q), out_send.at[q], out_recv.at[q])
    for copy in pending:
        copy.wait_send()


def on_device(L, R, source, to_modes, from_modes, eigenvalue, shifts, weights, neighbors):
    slab, nodes = source.shape
    S = weights.shape[0]
    levels = to_modes.shape[0]
    T, X, K = CHUNKS, R // CORES, slab * CORES
    half = nodes // CORES
    NB = half // BLOCK
    CW = half // T
    E = NB + 2 * HALO
    A = -(-S // GROUP)
    f32 = jnp.float32
    dma = pltpu.SemaphoreType.DMA
    vmem = pl.BlockSpec(memory_space=pltpu.VMEM)
    anywhere = pl.BlockSpec(memory_space=pl.ANY)
    smoothed, norm = pl.pallas_call(
        functools.partial(kernel, L, R, S),
        name="smoother",
        out_shape=(
            jax.ShapeDtypeStruct((slab, nodes), f32),
            jax.ShapeDtypeStruct((1, slab), f32),
        ),
        in_specs=[
            anywhere, anywhere, vmem, vmem, vmem, vmem, pl.BlockSpec(memory_space=pltpu.SMEM),
        ],
        out_specs=(anywhere, vmem),
        scratch_shapes=[
            pltpu.VMEM((T, levels, CW), f32),
            pltpu.VMEM((S, half), f32),
            pltpu.VMEM((NB, (A + 1) * GROUP, BLOCK), f32),
            pltpu.VMEM((A * E, K, BLOCK), f32),
            pltpu.VMEM((A * E, K, BLOCK), f32),
            pltpu.VMEM((X, NB, K, BLOCK), f32),
            pltpu.VMEM((X, NB, K, BLOCK), f32),
            pltpu.VMEM((levels, levels), f32),
            pltpu.VMEM((X, 2, K, BLOCK), f32),
            pltpu.VMEM((T, 2, slab, CW), f32),
            pltpu.VMEM((NB, BLOCK), f32),
            pltpu.VMEM((L, 8, BLOCK), f32),
            pltpu.VMEM((R, 8, BLOCK), f32),
            pltpu.VMEM((L, 8, BLOCK), f32),
            pltpu.VMEM((CORES, 8, BLOCK), f32),
            dma((T,)), dma(()),
            dma((T, R - 1)), dma((T, R)),
            dma((T,)), dma((T,)), dma((T,)), dma((T,)),
            dma((T, max(X - 1, 1))), dma((T, X)),
            dma((L - 1,)), dma((L,)), dma((R - 1,)), dma((R,)),
            dma((L - 1,)), dma((L,)), dma(()), dma(()),
            dma((T,)), dma((T,)), dma((T,)),
        ],
        compiler_params=pltpu.CompilerParams(
            collective_id=0, has_side_effects=True, vmem_limit_bytes=48 * 1024 * 1024
        ),
    )(
        source, weights, to_modes, from_modes, eigenvalue.reshape(1, levels),
        shifts.reshape(nodes // BLOCK, BLOCK), neighbors,
    )
    return smoothed, norm.reshape(slab)


def solution(mesh):
    return jax.shard_map(
        functools.partial(on_device, mesh.shape["lat"], mesh.shape["rad"]),
        mesh=mesh,
        in_specs=(P("rad", "lat"), P(), P(), P(), P("lat"), P(None, "lat"), P(None, "lat")),
        out_specs=(P("rad", "lat"), P("rad")),
        check_vma=False,
    )
```

```python
import functools

import jax
import jax.numpy as jnp
from jax import lax
from jax.experimental import pallas as pl
from jax.experimental.pallas import tpu as pltpu
from jax.sharding import PartitionSpec as P

BLOCK = 128
HALO = 8
CHUNKS = 4
GROUP = 8
CORES = 2
HIGHEST = lax.Precision.HIGHEST
MESH = pl.DeviceIdType.MESH


def dot(a, b):
    return jnp.dot(a, b, precision=HIGHEST, preferred_element_type=jnp.float32)


def kernel(
    L, R, S,
    src, w_hbm, to_hbm, from_hbm, eig_hbm, shift_hbm, nbr_hbm,
    out, res_ref,
    gathered, wv, wr, ext1, ext2, modal, image, eig_t, coef, part, rows, s1, s2, s3, s4,
    to_ref, from_ref, eig_ref, nbr_ref, in_sem, own_sem, w_sem, ag_send, ag_recv, h1_send, h1_recv, h2_send, h2_recv, im_send, im_recv,
    s1_send, s1_recv, s2_send, s2_recv, s3_send, s3_recv, s4_send, s4_recv,
    out_send, out_recv, out_sem,
):
    T = CHUNKS
    X = R // CORES
    slab, nodes = src.shape
    K = slab * CORES
    half = nodes // CORES
    NB = half // BLOCK
    CB = NB // T
    CW = CB * BLOCK
    E = NB + 2 * HALO
    A = -(-S // GROUP)
    lat = lax.axis_index("lat")
    rad = lax.axis_index("rad")
    core = lax.rem(rad, CORES)
    chip = lax.div(rad, CORES)
    partner = chip * CORES + (1 - core)
    left_lat = lax.rem(lat + (L - 1) * (1 - core), L)
    right_lat = lax.rem(lat + core, L)

    def order(t, c):
        return t * (1 - c) + (T - 1 - t) * c

    def own_copy(q):
        return pltpu.make_async_copy(
            src.at[:, pl.ds(pl.multiple_of(core * half + q * CW, BLOCK), CW)],
            gathered.at[q, pl.ds(pl.multiple_of(rad * slab, 8), slab), :],
            own_sem.at[q],
        )

    w_copy = pltpu.make_async_copy(
        w_hbm.at[:, pl.ds(pl.multiple_of(core * half, BLOCK), half)], wv, w_sem
    )
    inputs = [
        pltpu.make_async_copy(a, b, in_sem.at[i])
        for i, (a, b) in enumerate([
            (to_hbm, to_ref), (from_hbm, from_ref), (eig_hbm, eig_ref), (nbr_hbm, nbr_ref),
            (shift_hbm.at[pl.ds(pl.multiple_of(core * NB, 8), NB), :], rows),
        ])
    ]
    w_copy.start()
    for copy in inputs:
        copy.start()
    for q in range(T):
        own_copy(q).start()

    barrier = pltpu.get_barrier_semaphore()
    for j in range(1, R):
        pl.semaphore_signal(
            barrier, inc=1, device_id={"lat": lat, "rad": lax.rem(rad + j, R)}, device_id_type=MESH
        )
    other_lat = left_lat * (1 - core) + right_lat * core
    pl.semaphore_signal(
        barrier, inc=1, device_id={"lat": other_lat, "rad": partner}, device_id_type=MESH
    )
    for j in range(1, L):
        pl.semaphore_signal(
            barrier, inc=1, device_id={"lat": lax.rem(lat + j, L), "rad": rad}, device_id_type=MESH
        )
    pl.semaphore_wait(barrier, R - 1 + 1 + L - 1)

    pending = []

    def remote(src_ref, dst_ref, send, recv, lat_to, rad_to):
        copy = pltpu.make_async_remote_copy(
            src_ref=src_ref, dst_ref=dst_ref, send_sem=send, recv_sem=recv,
            device_id={"lat": lat_to, "rad": rad_to}, device_id_type=MESH,
        )
        copy.start()
        pending.append(copy)

    def arrived(dst_ref, send, recv):
        pltpu.make_async_remote_copy(
            src_ref=dst_ref, dst_ref=dst_ref, send_sem=send, recv_sem=recv,
            device_id={"lat": lat, "rad": partner}, device_id_type=MESH,
        ).wait_recv()

    def slot(q, r):
        return gathered.at[q, pl.ds(pl.multiple_of(r * slab, 8), slab), :]

    for t in range(T):
        for j in range(1, R):
            to = lax.rem(rad + j, R)
            to_core = lax.rem(to, CORES)
            q = order(t, to_core)
            remote(
                src.at[:, pl.ds(pl.multiple_of(to_core * half + q * CW, BLOCK), CW)],
                slot(q, rad), ag_send.at[t, j - 1], ag_recv.at[q, rad], lat, to,
            )

    w_copy.wait()
    for copy in inputs:
        copy.wait()
    row_id = lax.broadcasted_iota(jnp.int32, (A * GROUP, BLOCK), 0)

    def prepare(b, carry):
        wr[b, pl.ds((A - 1) * GROUP, GROUP), :] = jnp.zeros((GROUP, BLOCK), jnp.float32)
        wr[b, pl.ds(0, S), :] = wv[:, pl.ds(pl.multiple_of(b * BLOCK, BLOCK), BLOCK)]
        tile = wr[b, pl.ds(0, A * GROUP), :]
        placed = tile
        for c in range(1, GROUP):
            placed = jnp.where(lax.rem(row_id, GROUP) == c, pltpu.roll(tile, c, 1), placed)
        wr[b, pl.ds(0, A * GROUP), :] = placed
        diagonal = jnp.sum(tile, axis=0, keepdims=True) + rows[pl.ds(b, 1), :]
        wr[b, pl.ds(A * GROUP, GROUP), :] = jnp.broadcast_to(diagonal, (GROUP, BLOCK))
        return carry

    lax.fori_loop(0, NB, prepare, 0)
    levels = to_ref.shape[0]
    eig_t[...] = jnp.transpose(jnp.broadcast_to(eig_ref[...], (levels, levels)))
    eig = pl.ds(pl.multiple_of(chip * K, 8), K)

    def halo_send(buf, q, send, recv):
        upper = lax.div(q * 2, T)
        to_lat = left_lat * (1 - upper) + right_lat * upper
        at = HALO + q * CB
        dst = at + NB * (1 - upper) - NB * upper
        remote(
            buf.at[pl.ds(at, CB)], buf.at[pl.ds(dst, CB)], send.at[q], recv.at[q], to_lat, partner
        )

    def halo_wait(buf, send, recv):
        for q in range(T):
            dst = HALO + q * CB + (NB if q * 2 < T else -NB)
            arrived(buf.at[pl.ds(dst, CB)], send.at[q], recv.at[q])

    def spread(buf, k, value):
        for a in range(1, A):
            buf[a * E + k] = pltpu.roll(value, BLOCK - a * GROUP, 1)

    def spread_halo(buf):
        def step(k, carry):
            spread(buf, k, buf[k])
            spread(buf, k + NB + HALO, buf[k + NB + HALO])
            return carry

        lax.fori_loop(0, HALO, step, 0)

    own_rows = to_ref[pl.ds(pl.multiple_of(chip * K, 8), K), :]
    for t in range(T):
        q = order(t, core)
        own_copy(q).wait()
        for j in range(1, R):
            r = lax.rem(rad + j, R)
            arrived(slot(q, r), ag_send.at[t, j - 1], ag_recv.at[q, r])
        product = dot(own_rows, gathered[q])
        for i in range(CB):
            value = product[:, i * BLOCK:(i + 1) * BLOCK]
            ext1[HALO + q * CB + i] = value
            modal[chip, q * CB + i] = value
        halo_send(ext1, q, h1_send, h1_recv)
        for i in range(CB):
            spread(ext1, HALO + q * CB + i, product[:, i * BLOCK:(i + 1) * BLOCK])
    halo_wait(ext1, h1_send, h1_recv)
    spread_halo(ext1)

    def operate(buf, b, field):
        total = None
        for c in range(GROUP):
            inner = None
            for a in range(A):
                s = a * GROUP + c
                if s < S:
                    n = nbr_ref[s, core * NB + b]
                    term = buf[a * E + HALO + b + n] * wr[b, pl.ds(s, 1), :]
                    inner = term if inner is None else inner + term
            if inner is not None:
                moved = inner if c == 0 else pltpu.roll(inner, BLOCK - c, 1)
                total = moved if total is None else total + moved
        return (wr[b, pl.ds(A * GROUP, 1), :] + eig_t[eig, :]) * field - total

    zero = jnp.zeros((K, BLOCK), jnp.float32)
    sums = (zero, zero)
    for t in range(T):
        q = order(t, core)

        def first_pass(i, carry):
            b = q * CB + i
            field = ext1[HALO + b]
            value = operate(ext1, b, field)
            ext2[HALO + b] = value
            image[chip, b] = value
            return (carry[0] + field * field, carry[1] + value * value)

        sums = lax.fori_loop(0, CB, first_pass, sums)
        for j in range(1, X):
            to = lax.rem(chip + j, X)
            remote(
                image.at[chip, pl.ds(q * CB, CB)], image.at[chip, pl.ds(q * CB, CB)],
                im_send.at[t, j - 1], im_recv.at[q, chip], lat, to * CORES + core,
            )
        halo_send(ext2, q, h2_send, h2_recv)

    ones = jnp.ones((8, BLOCK), jnp.float32)

    def lanes(values):
        return lax.dot_general(
            ones, values, (((1,), (1,)), ((), ())), precision=HIGHEST,
            preferred_element_type=jnp.float32,
        )

    def lat_send(buf, send, recv):
        for j in range(1, L):
            remote(
                buf.at[lat], buf.at[lat], send.at[j - 1], recv.at[lat], lax.rem(lat + j, L), rad
            )

    def lat_sum(buf, send, recv):
        for j in range(1, L):
            l = lax.rem(lat + j, L)
            arrived(buf.at[l], send.at[j - 1], recv.at[l])
        total = buf[0]
        for l in range(1, L):
            total = total + buf[l]
        return total

    def put(buf, at, value):
        width = value.shape[1]
        if width < BLOCK:
            value = jnp.concatenate(
                [value, jnp.zeros((8, BLOCK - width), jnp.float32)], axis=1
            )
        buf[at] = value

    put(s1, lat, lanes(jnp.concatenate(sums, axis=0)))
    lat_send(s1, s1_send, s1_recv)

    for j in range(1, X):
        other = lax.rem(chip + j, X)
        other_rows = to_ref[pl.ds(pl.multiple_of(other * K, 8), K), :]
        for q in range(T):
            product = dot(other_rows, gathered[q])
            for i in range(CB):
                modal[other, q * CB + i] = product[:, i * BLOCK:(i + 1) * BLOCK]

    s2[rad] = lat_sum(s1, s1_send, s1_recv)
    for j in range(1, R):
        remote(
            s2.at[rad], s2.at[rad], s2_send.at[j - 1], s2_recv.at[rad], lat, lax.rem(rad + j, R)
        )
    for j in range(1, R):
        r = lax.rem(rad + j, R)
        arrived(s2.at[r], s2_send.at[j - 1], s2_recv.at[r])
    for x in range(X):
        line = s2[CORES * x]
        for c in range(1, CORES):
            line = line + s2[CORES * x + c]
        column = jnp.transpose(jnp.broadcast_to(line[0:1, :], (BLOCK, BLOCK)))
        base, power = column[0:K], column[K:2 * K]
        upper = 1.5 * jnp.sqrt(power / (base + 1e-06))
        lower = upper * 0.125
        center = (upper + lower) * 0.5
        half_width = (upper - lower) * 0.5
        sigma = center / half_width
        rho_zero = 1.0 / sigma
        rho_one = 1.0 / (2.0 * sigma - rho_zero)
        second = 2.0 * rho_one / half_width
        coef[x, 0] = (1.0 + rho_one * rho_zero) / center + second
        coef[x, 1] = -second / center

    mine = jnp.concatenate(
        [
            from_ref[pl.ds(pl.multiple_of(rad * slab, 8), slab), :],
            from_ref[pl.ds(pl.multiple_of(partner * slab, 8), slab), :],
        ],
        axis=0,
    )

    def columns(q):
        return out.at[:, pl.ds(pl.multiple_of(core * half + q * CW, BLOCK), CW)]

    def their_columns(q):
        return out.at[:, pl.ds(pl.multiple_of((1 - core) * half + q * CW, BLOCK), CW)]

    def finish(t):
        q = order(t, core)
        for j in range(1, X):
            x = lax.rem(chip + j, X)
            arrived(image.at[x, pl.ds(q * CB, CB)], im_send.at[t, j - 1], im_recv.at[q, x])
        blocks = []
        for i in range(CB):
            b = q * CB + i
            blocks.append(
                jnp.concatenate(
                    [coef[x, 0] * modal[x, b] + coef[x, 1] * image[x, b] for x in range(X)], axis=0
                )
            )
        product = dot(mine, jnp.concatenate(blocks, axis=1))
        part[q, 0] = product[0:slab]
        part[q, 1] = product[slab:K]
        remote(part.at[q, 1], columns(q), out_send.at[q], out_recv.at[q], lat, partner)
        pltpu.make_async_copy(part.at[q, 0], columns(q), out_sem.at[q]).start()

    finish(0)

    halo_wait(ext2, h2_send, h2_recv)
    spread_halo(ext2)

    def spread_own(b, carry):
        spread(ext2, HALO + b, ext2[HALO + b])
        return carry

    lax.fori_loop(0, NB, spread_own, 0)

    def second_pass(b, carry):
        field = ext2[HALO + b]
        value = operate(ext2, b, field)
        final = modal[chip, b] - (coef[chip, 0] * field + coef[chip, 1] * value)
        return carry + final * final

    squares = lax.fori_loop(0, NB, second_pass, zero)
    put(s3, lat, lanes(squares))
    lat_send(s3, s3_send, s3_recv)

    for t in range(1, T):
        finish(t)

    s4[core] = lat_sum(s3, s3_send, s3_recv)
    remote(s4.at[core], s4.at[core], s4_send, s4_recv, lat, partner)
    arrived(s4.at[1 - core], s4_send, s4_recv)
    base_line = s2[CORES * chip] + s2[CORES * chip + 1]
    norm = jnp.sqrt((s4[0] + s4[1]) / (base_line + 1e-06))
    res_ref[...] = jnp.where(core == 0, norm[0:1, 0:slab], norm[0:1, slab:2 * slab])

    for q in range(T):
        pltpu.make_async_copy(part.at[q, 0], columns(q), out_sem.at[q]).wait()
        arrived(their_columns(q), out_send.at[q], out_recv.at[q])
    for copy in pending:
        copy.wait_send()


def on_device(L, R, source, to_modes, from_modes, eigenvalue, shifts, weights, neighbors):
    slab, nodes = source.shape
    S = weights.shape[0]
    levels = to_modes.shape[0]
    T, X, K = CHUNKS, R // CORES, slab * CORES
    half = nodes // CORES
    NB = half // BLOCK
    CW = half // T
    E = NB + 2 * HALO
    A = -(-S // GROUP)
    f32 = jnp.float32
    dma = pltpu.SemaphoreType.DMA
    vmem = pl.BlockSpec(memory_space=pltpu.VMEM)
    hbm = pl.BlockSpec(memory_space=pltpu.HBM)
    smoothed, norm = pl.pallas_call(
        functools.partial(kernel, L, R, S),
        name="smoother",
        out_shape=(
            jax.ShapeDtypeStruct((slab, nodes), f32),
            jax.ShapeDtypeStruct((1, slab), f32),
        ),
        in_specs=[hbm] * 7,
        out_specs=(hbm, vmem),
        scratch_shapes=[
            pltpu.VMEM((T, levels, CW), f32),
            pltpu.VMEM((S, half), f32),
            pltpu.VMEM((NB, (A + 1) * GROUP, BLOCK), f32),
            pltpu.VMEM((A * E, K, BLOCK), f32),
            pltpu.VMEM((A * E, K, BLOCK), f32),
            pltpu.VMEM((X, NB, K, BLOCK), f32),
            pltpu.VMEM((X, NB, K, BLOCK), f32),
            pltpu.VMEM((levels, levels), f32),
            pltpu.VMEM((X, 2, K, BLOCK), f32),
            pltpu.VMEM((T, 2, slab, CW), f32),
            pltpu.VMEM((NB, BLOCK), f32),
            pltpu.VMEM((L, 8, BLOCK), f32),
            pltpu.VMEM((R, 8, BLOCK), f32),
            pltpu.VMEM((L, 8, BLOCK), f32),
            pltpu.VMEM((CORES, 8, BLOCK), f32),
            pltpu.VMEM((levels, levels), f32),
            pltpu.VMEM((levels, levels), f32),
            pltpu.VMEM((1, levels), f32),
            pltpu.SMEM(neighbors.shape, jnp.int32),
            dma((5,)), dma((T,)), dma(()),
            dma((T, R - 1)), dma((T, R)),
            dma((T,)), dma((T,)), dma((T,)), dma((T,)),
            dma((T, max(X - 1, 1))), dma((T, X)),
            dma((L - 1,)), dma((L,)), dma((R - 1,)), dma((R,)),
            dma((L - 1,)), dma((L,)), dma(()), dma(()),
            dma((T,)), dma((T,)), dma((T,)),
        ],
        compiler_params=pltpu.CompilerParams(
            collective_id=0, has_side_effects=True, vmem_limit_bytes=67043328
        ),
    )(
        source, weights, to_modes, from_modes, eigenvalue.reshape(1, levels),
        shifts.reshape(nodes // BLOCK, BLOCK), neighbors,
    )
    return smoothed, norm.reshape(slab)


def solution(mesh):
    return jax.shard_map(
        functools.partial(on_device, mesh.shape["lat"], mesh.shape["rad"]),
        mesh=mesh,
        in_specs=(P("rad", "lat"), P(), P(), P(), P("lat"), P(None, "lat"), P(None, "lat")),
        out_specs=(P("rad", "lat"), P("rad")),
        check_vma=False,
    )
```

```python
import functools

import jax
import jax.numpy as jnp
from jax import lax
from jax.experimental import pallas as pl
from jax.experimental.pallas import tpu as pltpu
from jax.sharding import PartitionSpec as P

BLOCK = 128
HALO = 8
CHUNKS = 4
GROUP = 8
CORES = 2
HIGHEST = lax.Precision.HIGHEST
MESH = pl.DeviceIdType.MESH


def dot(a, b):
    return jnp.dot(a, b, precision=HIGHEST, preferred_element_type=jnp.float32)


def kernel(
    L, R, S,
    src, w_hbm, to_hbm, from_hbm, eig_hbm, shift_hbm, nbr_hbm,
    out, res_ref,
    gathered, wv, wr, outer1, inner1, outer2, inner2, others, modal, image, eig_t, coef, part,
    rows, s1, s2, s3, to_ref, from_ref, eig_ref, nbr_ref,
    in_sem, own_sem, w_sem, ag_send, ag_recv,
    o1_send, o1_recv, i1_send, i1_recv, o2_send, o2_recv, i2_send, i2_recv, x_send, x_recv,
    im_send, im_recv, s1_send, s1_recv, s2_send, s2_recv, s3_send, s3_recv,
    out_send, out_recv, out_sem,
):
    T = CHUNKS
    X = R // CORES
    M = L * CORES
    slab, nodes = src.shape
    K = slab * CORES
    half = nodes // CORES
    NB = half // BLOCK
    CB = NB // T
    HC = HALO // CB
    CW = CB * BLOCK
    E = NB + HALO
    A = -(-S // GROUP)
    lat = lax.axis_index("lat")
    rad = lax.axis_index("rad")
    core = lax.rem(rad, CORES)
    chip = lax.div(rad, CORES)
    partner = chip * CORES + (1 - core)
    me = lat * CORES + core
    other_lat = lax.rem(lat + (L - 1) * (1 - core) + core, L)

    def order(t, c):
        return t * (1 - c) + (T - 1 - t) * c

    def own_copy(q):
        return pltpu.make_async_copy(
            src.at[:, pl.ds(pl.multiple_of(core * half + q * CW, BLOCK), CW)],
            gathered.at[q, pl.ds(pl.multiple_of(rad * slab, 8), slab), :],
            own_sem.at[q],
        )

    w_copy = pltpu.make_async_copy(
        w_hbm.at[:, pl.ds(pl.multiple_of(core * half, BLOCK), half)], wv, w_sem
    )
    inputs = [
        pltpu.make_async_copy(a, b, in_sem.at[i])
        for i, (a, b) in enumerate([
            (to_hbm, to_ref), (from_hbm, from_ref), (eig_hbm, eig_ref), (nbr_hbm, nbr_ref),
            (shift_hbm.at[pl.ds(pl.multiple_of(core * NB, 8), NB), :], rows),
        ])
    ]

    def plane_peer(j):
        m = lax.rem(me + j, M)
        return m, lax.div(m, CORES), chip * CORES + lax.rem(m, CORES)

    barrier = pltpu.get_barrier_semaphore()
    for j in range(1, R):
        r = lax.rem(rad + j, R)
        pl.semaphore_signal(
            barrier, inc=1, device_id={"lat": lat, "rad": r}, device_id_type=MESH
        )
    for j in range(1, M):
        m, to_lat, to_rad = plane_peer(j)
        pl.semaphore_signal(
            barrier, inc=1, device_id={"lat": to_lat, "rad": to_rad}, device_id_type=MESH
        )
    w_copy.start()
    for copy in inputs:
        copy.start()
    for q in range(T):
        own_copy(q).start()
    pl.semaphore_wait(barrier, R - 1 + M - 1)

    pending = []

    def remote(src_ref, dst_ref, send, recv, lat_to, rad_to):
        copy = pltpu.make_async_remote_copy(
            src_ref=src_ref, dst_ref=dst_ref, send_sem=send, recv_sem=recv,
            device_id={"lat": lat_to, "rad": rad_to}, device_id_type=MESH,
        )
        copy.start()
        pending.append(copy)

    def arrived(dst_ref, send, recv):
        pltpu.make_async_remote_copy(
            src_ref=dst_ref, dst_ref=dst_ref, send_sem=send, recv_sem=recv,
            device_id={"lat": lat, "rad": partner}, device_id_type=MESH,
        ).wait_recv()

    def slot(q, r):
        return gathered.at[q, pl.ds(pl.multiple_of(r * slab, 8), slab), :]

    for t in range(T):
        for j in range(1, R):
            to = lax.rem(rad + j, R)
            to_core = lax.rem(to, CORES)
            q = order(t, to_core)
            remote(
                src.at[:, pl.ds(pl.multiple_of(to_core * half + q * CW, BLOCK), CW)],
                slot(q, rad), ag_send.at[t, j - 1], ag_recv.at[q, rad], lat, to,
            )

    w_copy.wait()
    for copy in inputs:
        copy.wait()
    row_id = lax.broadcasted_iota(jnp.int32, (A * GROUP, BLOCK), 0)

    def prepare(b, carry):
        wr[b, pl.ds((A - 1) * GROUP, GROUP), :] = jnp.zeros((GROUP, BLOCK), jnp.float32)
        wr[b, pl.ds(0, S), :] = wv[:, pl.ds(pl.multiple_of(b * BLOCK, BLOCK), BLOCK)]
        tile = wr[b, pl.ds(0, A * GROUP), :]
        placed = tile
        for c in range(1, GROUP):
            placed = jnp.where(lax.rem(row_id, GROUP) == c, pltpu.roll(tile, c, 1), placed)
        wr[b, pl.ds(0, A * GROUP), :] = placed
        diagonal = jnp.sum(tile, axis=0, keepdims=True) + rows[pl.ds(b, 1), :]
        wr[b, pl.ds(A * GROUP, GROUP), :] = jnp.broadcast_to(diagonal, (GROUP, BLOCK))
        return carry

    lax.fori_loop(0, NB, prepare, 0)
    levels = to_ref.shape[0]
    eig_t[...] = jnp.transpose(jnp.broadcast_to(eig_ref[...], (levels, levels)))

    o_at = HALO * (1 - core)
    i_at = HALO * core

    def outer_dst(c, q):
        return (1 - c) * (NB + q * CB) + c * (q * CB - NB + HALO)

    def inner_dst(c, q):
        return c * (NB + q * CB) + (1 - c) * (q * CB - NB + HALO)

    def outer_send(buf, t, send, recv):
        q = order(t, core)
        remote(
            buf.at[pl.ds(o_at + q * CB, CB)], buf.at[pl.ds(outer_dst(core, q), CB)],
            send.at[t], recv.at[t], other_lat, partner,
        )

    def outer_wait(buf, send, recv):
        for t in range(HC):
            at = outer_dst(1 - core, order(t, 1 - core))
            arrived(buf.at[pl.ds(at, CB)], send.at[t], recv.at[t])

    def inner_send(buf, base, t, send, recv):
        q = order(t, core)
        remote(
            buf.at[pl.ds(base + i_at + q * CB, CB)],
            buf.at[pl.ds(base + inner_dst(core, q), CB)],
            send.at[t - (T - HC)], recv.at[t - (T - HC)], lat, partner,
        )

    def inner_wait(buf, base, send, recv):
        for t in range(T - HC, T):
            at = inner_dst(1 - core, order(t, 1 - core))
            arrived(buf.at[pl.ds(base + at, CB)], send.at[t - (T - HC)], recv.at[t - (T - HC)])

    def spread_at(targets, value):
        for a in range(1, A):
            moved = pltpu.roll(value, BLOCK - a * GROUP, 1)
            for buf, k in targets:
                buf[a * E + k] = moved

    def spread_halo(buf, base, at):
        def step(k, carry):
            spread_at([(buf, base + at + k)], buf[base + at + k])
            return carry

        lax.fori_loop(0, HALO, step, 0)

    outer_halo = core * NB
    inner_halo = (1 - core) * NB

    def own_rows(x):
        return to_ref[pl.ds(pl.multiple_of(x * K, 8), K), :]

    def project_others(t):
        q = order(t, core)
        for j in range(1, X):
            x = lax.rem(chip + j, X)
            base = (j - 1) * A * E
            product = dot(own_rows(x), gathered[q])
            for i in range(CB):
                value = product[:, i * BLOCK:(i + 1) * BLOCK]
                modal[x, q * CB + i] = value
                others[base + i_at + q * CB + i] = value
            if t >= T - HC:
                inner_send(others, base, t, x_send.at[j - 1], x_recv.at[j - 1])
            for i in range(CB):
                spread_at(
                    [(others, base + i_at + q * CB + i)], product[:, i * BLOCK:(i + 1) * BLOCK]
                )

    for t in range(T):
        q = order(t, core)
        own_copy(q).wait()
        for j in range(1, R):
            r = lax.rem(rad + j, R)
            arrived(slot(q, r), ag_send.at[t, j - 1], ag_recv.at[q, r])
        product = dot(own_rows(chip), gathered[q])
        for i in range(CB):
            value = product[:, i * BLOCK:(i + 1) * BLOCK]
            b = q * CB + i
            outer1[o_at + b] = value
            inner1[i_at + b] = value
            modal[chip, b] = value
        if t < HC:
            outer_send(outer1, t, o1_send, o1_recv)
        if t >= T - HC:
            inner_send(inner1, 0, t, i1_send, i1_recv)
        for i in range(CB):
            b = q * CB + i
            spread_at(
                [(outer1, o_at + b), (inner1, i_at + b)], product[:, i * BLOCK:(i + 1) * BLOCK]
            )
        if t < T - 1:
            project_others(t)
        if t == T - 2:
            outer_wait(outer1, o1_send, o1_recv)
            spread_halo(outer1, 0, outer_halo)

    def operate(buf, base, x, b, field):
        total = None
        for c in range(GROUP):
            inner = None
            for a in range(A):
                s = a * GROUP + c
                if s < S:
                    n = nbr_ref[s, core * NB + b]
                    term = buf[base + a * E + b + n] * wr[b, pl.ds(s, 1), :]
                    inner = term if inner is None else inner + term
            if inner is not None:
                moved = inner if c == 0 else pltpu.roll(inner, BLOCK - c, 1)
                total = moved if total is None else total + moved
        eig = eig_t[pl.ds(pl.multiple_of(x * K, 8), K), :]
        return (wr[b, pl.ds(A * GROUP, 1), :] + eig) * field - total

    def first_pass(buf, at):
        def step(b, carry):
            field = modal[chip, b]
            value = operate(buf, at, chip, b, field)
            outer2[o_at + b] = value
            inner2[i_at + b] = value
            image[chip, b] = value
            return (carry[0] + field * field, carry[1] + value * value)

        return step

    zero = jnp.zeros((K, BLOCK), jnp.float32)
    sums = (zero, zero)
    for t in range(T):
        q = order(t, core)
        if t == T // 2:
            inner_wait(inner1, 0, i1_send, i1_recv)
            spread_halo(inner1, 0, inner_halo)
        step = first_pass(outer1, o_at) if t < T // 2 else first_pass(inner1, i_at)
        sums = lax.fori_loop(q * CB, (q + 1) * CB, step, sums)
        if t < HC:
            outer_send(outer2, t, o2_send, o2_recv)
        if t < T // 2:
            for j in range(1, X):
                to = lax.rem(chip + j, X)
                remote(
                    image.at[chip, pl.ds(q * CB, CB)], image.at[chip, pl.ds(q * CB, CB)],
                    im_send.at[t, j - 1], im_recv.at[q, chip], lat, to * CORES + core,
                )
        if t >= T - HC:
            inner_send(inner2, 0, t, i2_send, i2_recv)

    ones = jnp.ones((8, BLOCK), jnp.float32)

    def lanes(values):
        line = lax.dot_general(
            ones, values, (((1,), (1,)), ((), ())), precision=HIGHEST,
            preferred_element_type=jnp.float32,
        )
        width = line.shape[1]
        if width < BLOCK:
            line = jnp.concatenate(
                [line, jnp.zeros((8, BLOCK - width), jnp.float32)], axis=1
            )
        return line[0:1]

    def plane_send(buf, send, recv):
        for j in range(1, M):
            m, to_lat, to_rad = plane_peer(j)
            remote(buf.at[me], buf.at[me], send.at[j - 1], recv.at[me], to_lat, to_rad)

    def plane_sum(buf, send, recv):
        for j in range(1, M):
            m = lax.rem(me + j, M)
            arrived(buf.at[m], send.at[j - 1], recv.at[m])
        total = buf[0]
        for m in range(1, M):
            total = total + buf[m]
        return total

    s1[me] = lanes(jnp.concatenate(sums, axis=0))
    plane_send(s1, s1_send, s1_recv)
    project_others(T - 1)

    s2[chip] = plane_sum(s1, s1_send, s1_recv)
    for j in range(1, X):
        x = lax.rem(chip + j, X)
        remote(
            s2.at[chip], s2.at[chip], s2_send.at[j - 1], s2_recv.at[chip], lat, x * CORES + core
        )

    inside = (NB // 2) * (1 - core)
    for j in range(1, X):
        x = lax.rem(chip + j, X)
        base = (j - 1) * A * E
        inner_wait(others, base, x_send.at[j - 1], x_recv.at[j - 1])
        spread_halo(others, base, inner_halo)
    for j in range(1, X):
        x = lax.rem(chip + j, X)
        base = (j - 1) * A * E

        def others_pass(b, carry, x=x, base=base):
            image[x, b] = operate(others, base + i_at, x, b, modal[x, b])
            return carry

        lax.fori_loop(inside, inside + NB // 2, others_pass, 0)

    for j in range(1, X):
        x = lax.rem(chip + j, X)
        arrived(s2.at[x], s2_send.at[j - 1], s2_recv.at[x])
    for x in range(X):
        column = jnp.transpose(jnp.broadcast_to(s2[x], (BLOCK, BLOCK)))
        base, power = column[0:K], column[K:2 * K]
        upper = 1.5 * jnp.sqrt(power / (base + 1e-06))
        lower = upper * 0.125
        center = (upper + lower) * 0.5
        half_width = (upper - lower) * 0.5
        sigma = center / half_width
        rho_zero = 1.0 / sigma
        rho_one = 1.0 / (2.0 * sigma - rho_zero)
        second = 2.0 * rho_one / half_width
        coef[x, 0] = (1.0 + rho_one * rho_zero) / center + second
        coef[x, 1] = -second / center

    mine = jnp.concatenate(
        [
            from_ref[pl.ds(pl.multiple_of(rad * slab, 8), slab), :],
            from_ref[pl.ds(pl.multiple_of(partner * slab, 8), slab), :],
        ],
        axis=0,
    )

    def columns(q):
        return out.at[:, pl.ds(pl.multiple_of(core * half + q * CW, BLOCK), CW)]

    def their_columns(q):
        return out.at[:, pl.ds(pl.multiple_of((1 - core) * half + q * CW, BLOCK), CW)]

    def finish(t):
        q = order(t, core)
        if t < T // 2:
            for j in range(1, X):
                x = lax.rem(chip + j, X)
                arrived(image.at[x, pl.ds(q * CB, CB)], im_send.at[t, j - 1], im_recv.at[q, x])
        blocks = []
        for i in range(CB):
            b = q * CB + i
            blocks.append(
                jnp.concatenate(
                    [coef[x, 0] * modal[x, b] + coef[x, 1] * image[x, b] for x in range(X)], axis=0
                )
            )
        product = dot(mine, jnp.concatenate(blocks, axis=1))
        part[q, 0] = product[0:slab]
        part[q, 1] = product[slab:K]
        remote(part.at[q, 1], columns(q), out_send.at[q], out_recv.at[q], lat, partner)
        pltpu.make_async_copy(part.at[q, 0], columns(q), out_sem.at[q]).start()

    def second_pass(buf, at):
        def step(b, carry):
            field = image[chip, b]
            value = operate(buf, at, chip, b, field)
            final = modal[chip, b] - (coef[chip, 0] * field + coef[chip, 1] * value)
            return carry + final * final

        return step

    def spread_own(b, carry):
        spread_at([(outer2, o_at + b), (inner2, i_at + b)], image[chip, b])
        return carry

    lax.fori_loop(0, NB, spread_own, 0)
    inner_wait(inner2, 0, i2_send, i2_recv)
    spread_halo(inner2, 0, inner_halo)
    squares = lax.fori_loop(inside, inside + NB // 2, second_pass(inner2, i_at), zero)
    for t in range(T // 2, T):
        finish(t)
    finish(0)

    outer_wait(outer2, o2_send, o2_recv)
    spread_halo(outer2, 0, outer_halo)
    outside = (NB // 2) * core
    squares = lax.fori_loop(outside, outside + NB // 2, second_pass(outer2, o_at), squares)
    s3[me] = lanes(squares)
    plane_send(s3, s3_send, s3_recv)
    for t in range(1, T // 2):
        finish(t)

    norm = jnp.sqrt(plane_sum(s3, s3_send, s3_recv) / (s2[chip] + 1e-06))
    res_ref[...] = jnp.where(core == 0, norm[:, 0:slab], norm[:, slab:2 * slab])

    for q in range(T):
        pltpu.make_async_copy(part.at[q, 0], columns(q), out_sem.at[q]).wait()
        arrived(their_columns(q), out_send.at[q], out_recv.at[q])
    for copy in pending:
        copy.wait_send()


def on_device(L, R, source, to_modes, from_modes, eigenvalue, shifts, weights, neighbors):
    slab, nodes = source.shape
    S = weights.shape[0]
    levels = to_modes.shape[0]
    T, X, K = CHUNKS, R // CORES, slab * CORES
    half = nodes // CORES
    NB = half // BLOCK
    CW = half // T
    E = NB + HALO
    A = -(-S // GROUP)
    M = L * CORES
    HC = HALO // (NB // T)
    f32 = jnp.float32

    def window(count):
        return pltpu.VMEM((count * A * E, K, BLOCK), f32)

    dma = pltpu.SemaphoreType.DMA
    vmem = pl.BlockSpec(memory_space=pltpu.VMEM)
    hbm = pl.BlockSpec(memory_space=pltpu.HBM)
    smoothed, norm = pl.pallas_call(
        functools.partial(kernel, L, R, S),
        name="smoother",
        out_shape=(
            jax.ShapeDtypeStruct((slab, nodes), f32),
            jax.ShapeDtypeStruct((1, slab), f32),
        ),
        in_specs=[hbm] * 7,
        out_specs=(hbm, vmem),
        scratch_shapes=[
            pltpu.VMEM((T, levels, CW), f32),
            pltpu.VMEM((S, half), f32),
            pltpu.VMEM((NB, (A + 1) * GROUP, BLOCK), f32),
            window(1), window(1), window(1), window(1), window(X - 1),
            pltpu.VMEM((X, NB, K, BLOCK), f32),
            pltpu.VMEM((X, NB, K, BLOCK), f32),
            pltpu.VMEM((levels, levels), f32),
            pltpu.VMEM((X, 2, K, BLOCK), f32),
            pltpu.VMEM((T, 2, slab, CW), f32),
            pltpu.VMEM((NB, BLOCK), f32),
            pltpu.VMEM((M, 1, BLOCK), f32),
            pltpu.VMEM((X, 1, BLOCK), f32),
            pltpu.VMEM((M, 1, BLOCK), f32),
            pltpu.VMEM((levels, levels), f32),
            pltpu.VMEM((levels, levels), f32),
            pltpu.VMEM((1, levels), f32),
            pltpu.SMEM(neighbors.shape, jnp.int32),
            dma((5,)), dma((T,)), dma(()),
            dma((T, R - 1)), dma((T, R)),
            *[dma((HC,)) for _ in range(8)],
            dma((X - 1, HC)), dma((X - 1, HC)),
            dma((T, X - 1)), dma((T, X)),
            dma((M - 1,)), dma((M,)), dma((X - 1,)), dma((X,)),
            dma((M - 1,)), dma((M,)),
            dma((T,)), dma((T,)), dma((T,)),
        ],
        compiler_params=pltpu.CompilerParams(
            collective_id=0, has_side_effects=True, vmem_limit_bytes=67043328
        ),
    )(
        source, weights, to_modes, from_modes, eigenvalue.reshape(1, levels),
        shifts.reshape(nodes // BLOCK, BLOCK), neighbors,
    )
    return smoothed, norm.reshape(slab)


def solution(mesh):
    return jax.shard_map(
        functools.partial(on_device, mesh.shape["lat"], mesh.shape["rad"]),
        mesh=mesh,
        in_specs=(P("rad", "lat"), P(), P(), P(), P("lat"), P(None, "lat"), P(None, "lat")),
        out_specs=(P("rad", "lat"), P("rad")),
        check_vma=False,
    )
```

```python
import functools

import jax
import jax.numpy as jnp
from jax import lax
from jax.experimental import pallas as pl
from jax.experimental.pallas import tpu as pltpu
from jax.sharding import PartitionSpec as P

BLOCK = 128
HALO = 8
CHUNKS = 4
GROUP = 8
CORES = 2
HIGHEST = lax.Precision.HIGHEST
MESH = pl.DeviceIdType.MESH


def dot(a, b):
    return jnp.dot(a, b, precision=HIGHEST, preferred_element_type=jnp.float32)


def kernel(
    L, R, S,
    src, w_hbm, to_hbm, from_hbm, eig_hbm, shift_hbm, nbr_hbm,
    out, res_ref,
    gathered, wv, wr, outer1, inner1, outer2, inner2, others, modal, image, twice, eig_t, coef, part,
    rows, s1, s2, s3, to_ref, from_ref, eig_ref, nbr_ref,
    in_sem, own_sem, w_sem, ag_send, ag_recv,
    o1_send, o1_recv, i1_send, i1_recv, o2_send, o2_recv, i2_send, i2_recv, x_send, x_recv,
    im_send, im_recv, s1_send, s1_recv, s2_send, s2_recv, s3_send, s3_recv,
    out_send, out_recv, out_sem,
):
    T = CHUNKS
    X = R // CORES
    M = L * CORES
    slab, nodes = src.shape
    K = slab * CORES
    half = nodes // CORES
    NB = half // BLOCK
    CB = NB // T
    HC = HALO // CB
    CW = CB * BLOCK
    E = NB + HALO
    A = -(-S // GROUP)
    lat = lax.axis_index("lat")
    rad = lax.axis_index("rad")
    core = lax.rem(rad, CORES)
    chip = lax.div(rad, CORES)
    partner = chip * CORES + (1 - core)
    me = lat * CORES + core
    other_lat = lax.rem(lat + (L - 1) * (1 - core) + core, L)

    def order(t, c):
        return t * (1 - c) + (T - 1 - t) * c

    def own_copy(q):
        return pltpu.make_async_copy(
            src.at[:, pl.ds(pl.multiple_of(core * half + q * CW, BLOCK), CW)],
            gathered.at[q, pl.ds(pl.multiple_of(rad * slab, 8), slab), :],
            own_sem.at[q],
        )

    w_copy = pltpu.make_async_copy(
        w_hbm.at[:, pl.ds(pl.multiple_of(core * half, BLOCK), half)], wv, w_sem
    )
    inputs = [
        pltpu.make_async_copy(a, b, in_sem.at[i])
        for i, (a, b) in enumerate([
            (to_hbm, to_ref), (from_hbm, from_ref), (eig_hbm, eig_ref), (nbr_hbm, nbr_ref),
            (shift_hbm.at[pl.ds(pl.multiple_of(core * NB, 8), NB), :], rows),
        ])
    ]

    def plane_peer(j):
        m = lax.rem(me + j, M)
        return m, lax.div(m, CORES), chip * CORES + lax.rem(m, CORES)

    barrier = pltpu.get_barrier_semaphore()
    for j in range(1, R):
        r = lax.rem(rad + j, R)
        pl.semaphore_signal(
            barrier, inc=1, device_id={"lat": lat, "rad": r}, device_id_type=MESH
        )
    for j in range(1, M):
        m, to_lat, to_rad = plane_peer(j)
        pl.semaphore_signal(
            barrier, inc=1, device_id={"lat": to_lat, "rad": to_rad}, device_id_type=MESH
        )
    w_copy.start()
    for copy in inputs:
        copy.start()
    for q in range(T):
        own_copy(q).start()
    pl.semaphore_wait(barrier, R - 1 + M - 1)

    pending = []

    def remote(src_ref, dst_ref, send, recv, lat_to, rad_to):
        copy = pltpu.make_async_remote_copy(
            src_ref=src_ref, dst_ref=dst_ref, send_sem=send, recv_sem=recv,
            device_id={"lat": lat_to, "rad": rad_to}, device_id_type=MESH,
        )
        copy.start()
        pending.append(copy)

    def arrived(dst_ref, send, recv):
        pltpu.make_async_remote_copy(
            src_ref=dst_ref, dst_ref=dst_ref, send_sem=send, recv_sem=recv,
            device_id={"lat": lat, "rad": partner}, device_id_type=MESH,
        ).wait_recv()

    def slot(q, r):
        return gathered.at[q, pl.ds(pl.multiple_of(r * slab, 8), slab), :]

    for t in range(T):
        for j in range(1, R):
            to = lax.rem(rad + j, R)
            to_core = lax.rem(to, CORES)
            q = order(t, to_core)
            remote(
                src.at[:, pl.ds(pl.multiple_of(to_core * half + q * CW, BLOCK), CW)],
                slot(q, rad), ag_send.at[t, j - 1], ag_recv.at[q, rad], lat, to,
            )

    w_copy.wait()
    for copy in inputs:
        copy.wait()
    row_id = lax.broadcasted_iota(jnp.int32, (A * GROUP, BLOCK), 0)

    def prepare(b, carry):
        wr[b, pl.ds((A - 1) * GROUP, GROUP), :] = jnp.zeros((GROUP, BLOCK), jnp.float32)
        wr[b, pl.ds(0, S), :] = wv[:, pl.ds(pl.multiple_of(b * BLOCK, BLOCK), BLOCK)]
        tile = wr[b, pl.ds(0, A * GROUP), :]
        placed = tile
        for c in range(1, GROUP):
            placed = jnp.where(lax.rem(row_id, GROUP) == c, pltpu.roll(tile, c, 1), placed)
        wr[b, pl.ds(0, A * GROUP), :] = placed
        diagonal = jnp.sum(tile, axis=0, keepdims=True) + rows[pl.ds(b, 1), :]
        wr[b, pl.ds(A * GROUP, GROUP), :] = jnp.broadcast_to(diagonal, (GROUP, BLOCK))
        return carry

    lax.fori_loop(0, NB, prepare, 0)
    levels = to_ref.shape[0]
    eig_t[...] = jnp.transpose(jnp.broadcast_to(eig_ref[...], (levels, levels)))

    o_at = HALO * (1 - core)
    i_at = HALO * core

    def outer_dst(c, q):
        return (1 - c) * (NB + q * CB) + c * (q * CB - NB + HALO)

    def inner_dst(c, q):
        return c * (NB + q * CB) + (1 - c) * (q * CB - NB + HALO)

    def outer_send(buf, t, send, recv):
        q = order(t, core)
        remote(
            buf.at[pl.ds(o_at + q * CB, CB)], buf.at[pl.ds(outer_dst(core, q), CB)],
            send.at[t], recv.at[t], other_lat, partner,
        )

    def outer_wait(buf, send, recv):
        for t in range(HC):
            at = outer_dst(1 - core, order(t, 1 - core))
            arrived(buf.at[pl.ds(at, CB)], send.at[t], recv.at[t])

    def inner_send(buf, base, t, send, recv):
        q = order(t, core)
        remote(
            buf.at[pl.ds(base + i_at + q * CB, CB)],
            buf.at[pl.ds(base + inner_dst(core, q), CB)],
            send.at[t - (T - HC)], recv.at[t - (T - HC)], lat, partner,
        )

    def inner_wait(buf, base, send, recv):
        for t in range(T - HC, T):
            at = inner_dst(1 - core, order(t, 1 - core))
            arrived(buf.at[pl.ds(base + at, CB)], send.at[t - (T - HC)], recv.at[t - (T - HC)])

    def spread_at(targets, value):
        for a in range(1, A):
            moved = pltpu.roll(value, BLOCK - a * GROUP, 1)
            for buf, k in targets:
                buf[a * E + k] = moved

    def spread_halo(buf, base, at):
        def step(k, carry):
            spread_at([(buf, base + at + k)], buf[base + at + k])
            return carry

        lax.fori_loop(0, HALO, step, 0)

    outer_halo = core * NB
    inner_halo = (1 - core) * NB

    def own_rows(x):
        return to_ref[pl.ds(pl.multiple_of(x * K, 8), K), :]

    def project_others(t):
        q = order(t, core)
        for j in range(1, X):
            x = lax.rem(chip + j, X)
            base = (j - 1) * A * E
            product = dot(own_rows(x), gathered[q])
            for i in range(CB):
                value = product[:, i * BLOCK:(i + 1) * BLOCK]
                modal[x, q * CB + i] = value
                others[base + i_at + q * CB + i] = value
            if t >= T - HC:
                inner_send(others, base, t, x_send.at[j - 1], x_recv.at[j - 1])
            for i in range(CB):
                spread_at(
                    [(others, base + i_at + q * CB + i)], product[:, i * BLOCK:(i + 1) * BLOCK]
                )

    for t in range(T):
        q = order(t, core)
        own_copy(q).wait()
        for j in range(1, R):
            r = lax.rem(rad + j, R)
            arrived(slot(q, r), ag_send.at[t, j - 1], ag_recv.at[q, r])
        product = dot(own_rows(chip), gathered[q])
        for i in range(CB):
            value = product[:, i * BLOCK:(i + 1) * BLOCK]
            b = q * CB + i
            outer1[o_at + b] = value
            inner1[i_at + b] = value
            modal[chip, b] = value
        if t < HC:
            outer_send(outer1, t, o1_send, o1_recv)
        if t >= T - HC:
            inner_send(inner1, 0, t, i1_send, i1_recv)
        for i in range(CB):
            b = q * CB + i
            spread_at(
                [(outer1, o_at + b), (inner1, i_at + b)], product[:, i * BLOCK:(i + 1) * BLOCK]
            )
        if t < T - 1:
            project_others(t)
        if t == T - 2:
            outer_wait(outer1, o1_send, o1_recv)
            spread_halo(outer1, 0, outer_halo)

    def operate(buf, base, x, b, field):
        total = None
        for c in range(GROUP):
            inner = None
            for a in range(A):
                s = a * GROUP + c
                if s < S:
                    n = nbr_ref[s, core * NB + b]
                    term = buf[base + a * E + b + n] * wr[b, pl.ds(s, 1), :]
                    inner = term if inner is None else inner + term
            if inner is not None:
                moved = inner if c == 0 else pltpu.roll(inner, BLOCK - c, 1)
                total = moved if total is None else total + moved
        eig = eig_t[pl.ds(pl.multiple_of(x * K, 8), K), :]
        return (wr[b, pl.ds(A * GROUP, 1), :] + eig) * field - total

    def first_pass(buf, at):
        def step(b, carry):
            field = modal[chip, b]
            value = operate(buf, at, chip, b, field)
            outer2[o_at + b] = value
            inner2[i_at + b] = value
            image[chip, b] = value
            return (carry[0] + field * field, carry[1] + value * value)

        return step

    zero = jnp.zeros((K, BLOCK), jnp.float32)
    sums = (zero, zero)
    for t in range(T):
        q = order(t, core)
        if t == T // 2:
            inner_wait(inner1, 0, i1_send, i1_recv)
            spread_halo(inner1, 0, inner_halo)
        step = first_pass(outer1, o_at) if t < T // 2 else first_pass(inner1, i_at)
        sums = lax.fori_loop(q * CB, (q + 1) * CB, step, sums)
        if t < HC:
            outer_send(outer2, t, o2_send, o2_recv)
        if t < T // 2:
            for j in range(1, X):
                to = lax.rem(chip + j, X)
                remote(
                    image.at[chip, pl.ds(q * CB, CB)], image.at[chip, pl.ds(q * CB, CB)],
                    im_send.at[t, j - 1], im_recv.at[q, chip], lat, to * CORES + core,
                )
        if t >= T - HC:
            inner_send(inner2, 0, t, i2_send, i2_recv)

    ones = jnp.ones((8, BLOCK), jnp.float32)

    def lanes(values):
        line = lax.dot_general(
            ones, values, (((1,), (1,)), ((), ())), precision=HIGHEST,
            preferred_element_type=jnp.float32,
        )
        width = line.shape[1]
        if width < BLOCK:
            line = jnp.concatenate(
                [line, jnp.zeros((8, BLOCK - width), jnp.float32)], axis=1
            )
        return line[0:1]

    def plane_send(buf, send, recv):
        for j in range(1, M):
            m, to_lat, to_rad = plane_peer(j)
            remote(buf.at[me], buf.at[me], send.at[j - 1], recv.at[me], to_lat, to_rad)

    def plane_sum(buf, send, recv):
        for j in range(1, M):
            m = lax.rem(me + j, M)
            arrived(buf.at[m], send.at[j - 1], recv.at[m])
        total = buf[0]
        for m in range(1, M):
            total = total + buf[m]
        return total

    s1[me] = lanes(jnp.concatenate(sums, axis=0))
    plane_send(s1, s1_send, s1_recv)
    project_others(T - 1)

    inside = (NB // 2) * (1 - core)
    for j in range(1, X):
        x = lax.rem(chip + j, X)
        base = (j - 1) * A * E
        inner_wait(others, base, x_send.at[j - 1], x_recv.at[j - 1])
        spread_halo(others, base, inner_halo)
    for j in range(1, X):
        x = lax.rem(chip + j, X)
        base = (j - 1) * A * E

        def others_pass(b, carry, x=x, base=base):
            image[x, b] = operate(others, base + i_at, x, b, modal[x, b])
            return carry

        lax.fori_loop(inside, inside + NB // 2, others_pass, 0)

    mine = jnp.concatenate(
        [
            from_ref[pl.ds(pl.multiple_of(rad * slab, 8), slab), :],
            from_ref[pl.ds(pl.multiple_of(partner * slab, 8), slab), :],
        ],
        axis=0,
    )

    def columns(q):
        return out.at[:, pl.ds(pl.multiple_of(core * half + q * CW, BLOCK), CW)]

    def their_columns(q):
        return out.at[:, pl.ds(pl.multiple_of((1 - core) * half + q * CW, BLOCK), CW)]

    def finish(t):
        q = order(t, core)
        if t < T // 2:
            for j in range(1, X):
                x = lax.rem(chip + j, X)
                arrived(image.at[x, pl.ds(q * CB, CB)], im_send.at[t, j - 1], im_recv.at[q, x])
        blocks = []
        for i in range(CB):
            b = q * CB + i
            blocks.append(
                jnp.concatenate(
                    [coef[x, 0] * modal[x, b] + coef[x, 1] * image[x, b] for x in range(X)], axis=0
                )
            )
        product = dot(mine, jnp.concatenate(blocks, axis=1))
        part[q, 0] = product[0:slab]
        part[q, 1] = product[slab:K]
        remote(part.at[q, 1], columns(q), out_send.at[q], out_recv.at[q], lat, partner)
        pltpu.make_async_copy(part.at[q, 0], columns(q), out_sem.at[q]).start()

    def second_pass(buf, at):
        def step(b, carry):
            twice[b] = operate(buf, at, chip, b, image[chip, b])
            return carry

        return step

    def spread_own(b, carry):
        spread_at([(outer2, o_at + b), (inner2, i_at + b)], image[chip, b])
        return carry

    def residual(b, carry):
        final = modal[chip, b] - (coef[chip, 0] * image[chip, b] + coef[chip, 1] * twice[b])
        return carry + final * final

    lax.fori_loop(0, NB, spread_own, 0)
    inner_wait(inner2, 0, i2_send, i2_recv)
    spread_halo(inner2, 0, inner_halo)
    s2[chip] = plane_sum(s1, s1_send, s1_recv)
    for j in range(1, X):
        x = lax.rem(chip + j, X)
        remote(
            s2.at[chip], s2.at[chip], s2_send.at[j - 1], s2_recv.at[chip], lat, x * CORES + core
        )

    lax.fori_loop(inside, inside + NB // 2, second_pass(inner2, i_at), 0)
    outer_wait(outer2, o2_send, o2_recv)
    spread_halo(outer2, 0, outer_halo)
    outside = (NB // 2) * core
    lax.fori_loop(outside, outside + NB // 2, second_pass(outer2, o_at), 0)

    for j in range(1, X):
        x = lax.rem(chip + j, X)
        arrived(s2.at[x], s2_send.at[j - 1], s2_recv.at[x])
    for x in range(X):
        column = jnp.transpose(jnp.broadcast_to(s2[x], (BLOCK, BLOCK)))
        base, power = column[0:K], column[K:2 * K]
        upper = 1.5 * jnp.sqrt(power / (base + 1e-06))
        lower = upper * 0.125
        center = (upper + lower) * 0.5
        half_width = (upper - lower) * 0.5
        sigma = center / half_width
        rho_zero = 1.0 / sigma
        rho_one = 1.0 / (2.0 * sigma - rho_zero)
        second = 2.0 * rho_one / half_width
        coef[x, 0] = (1.0 + rho_one * rho_zero) / center + second
        coef[x, 1] = -second / center

    s3[me] = lanes(lax.fori_loop(0, NB, residual, zero))
    plane_send(s3, s3_send, s3_recv)
    for t in range(T // 2, T):
        finish(t)
    for t in range(T // 2):
        finish(t)

    norm = jnp.sqrt(plane_sum(s3, s3_send, s3_recv) / (s2[chip] + 1e-06))
    res_ref[...] = jnp.where(core == 0, norm[:, 0:slab], norm[:, slab:2 * slab])

    for q in range(T):
        pltpu.make_async_copy(part.at[q, 0], columns(q), out_sem.at[q]).wait()
        arrived(their_columns(q), out_send.at[q], out_recv.at[q])
    for copy in pending:
        copy.wait_send()


def on_device(L, R, source, to_modes, from_modes, eigenvalue, shifts, weights, neighbors):
    slab, nodes = source.shape
    S = weights.shape[0]
    levels = to_modes.shape[0]
    T, X, K = CHUNKS, R // CORES, slab * CORES
    half = nodes // CORES
    NB = half // BLOCK
    CW = half // T
    E = NB + HALO
    A = -(-S // GROUP)
    M = L * CORES
    HC = HALO // (NB // T)
    f32 = jnp.float32

    def window(count):
        return pltpu.VMEM((count * A * E, K, BLOCK), f32)

    dma = pltpu.SemaphoreType.DMA
    vmem = pl.BlockSpec(memory_space=pltpu.VMEM)
    hbm = pl.BlockSpec(memory_space=pltpu.HBM)
    smoothed, norm = pl.pallas_call(
        functools.partial(kernel, L, R, S),
        name="smoother",
        out_shape=(
            jax.ShapeDtypeStruct((slab, nodes), f32),
            jax.ShapeDtypeStruct((1, slab), f32),
        ),
        in_specs=[hbm] * 7,
        out_specs=(hbm, vmem),
        scratch_shapes=[
            pltpu.VMEM((T, levels, CW), f32),
            pltpu.VMEM((S, half), f32),
            pltpu.VMEM((NB, (A + 1) * GROUP, BLOCK), f32),
            window(1), window(1), window(1), window(1), window(X - 1),
            pltpu.VMEM((X, NB, K, BLOCK), f32),
            pltpu.VMEM((X, NB, K, BLOCK), f32),
            pltpu.VMEM((NB, K, BLOCK), f32),
            pltpu.VMEM((levels, levels), f32),
            pltpu.VMEM((X, 2, K, BLOCK), f32),
            pltpu.VMEM((T, 2, slab, CW), f32),
            pltpu.VMEM((NB, BLOCK), f32),
            pltpu.VMEM((M, 1, BLOCK), f32),
            pltpu.VMEM((X, 1, BLOCK), f32),
            pltpu.VMEM((M, 1, BLOCK), f32),
            pltpu.VMEM((levels, levels), f32),
            pltpu.VMEM((levels, levels), f32),
            pltpu.VMEM((1, levels), f32),
            pltpu.SMEM(neighbors.shape, jnp.int32),
            dma((5,)), dma((T,)), dma(()),
            dma((T, R - 1)), dma((T, R)),
            *[dma((HC,)) for _ in range(8)],
            dma((X - 1, HC)), dma((X - 1, HC)),
            dma((T, X - 1)), dma((T, X)),
            dma((M - 1,)), dma((M,)), dma((X - 1,)), dma((X,)),
            dma((M - 1,)), dma((M,)),
            dma((T,)), dma((T,)), dma((T,)),
        ],
        compiler_params=pltpu.CompilerParams(
            collective_id=0, has_side_effects=True, vmem_limit_bytes=67043328
        ),
    )(
        source, weights, to_modes, from_modes, eigenvalue.reshape(1, levels),
        shifts.reshape(nodes // BLOCK, BLOCK), neighbors,
    )
    return smoothed, norm.reshape(slab)


def solution(mesh):
    return jax.shard_map(
        functools.partial(on_device, mesh.shape["lat"], mesh.shape["rad"]),
        mesh=mesh,
        in_specs=(P("rad", "lat"), P(), P(), P(), P("lat"), P(None, "lat"), P(None, "lat")),
        out_specs=(P("rad", "lat"), P("rad")),
        check_vma=False,
    )
```
